32 devices in a mesh: leaf: 32 (over z, y, x, core).
Axes of the slice: x: 2, y: 2, z: 4, core: 2. Of those that a mesh axis runs over, the one named last changes fastest.
Arguments:
- coords: float32 [512, 3, 512], P('leaf'), may hold values from 0 to 1
- charges: float32 [512, 4, 512], P('leaf'), may hold values from -6 to 6
- bases: float32 [512, 64, 512], P('leaf'), may hold values from -0.25 to 0.25
- up_transfer: float32 [512, 64, 64], P('leaf'), may hold values from -0.25 to 0.25
- top_transfer: float32 [64, 64, 64], P('leaf'), may hold values from -0.75 to 0.75
- proxy_mid: float32 [64, 3, 64], replicated, may hold values from 0 to 1
- proxy_top: float32 [8, 3, 64], replicated, may hold values from 0 to 1
- near_list: int32 [512, 4], P('leaf'), may hold values from 0 to 511, as said below
- near_count: int32 [512], P('leaf'), may hold values from 1 to 4
- far_mid: int32 [64, 32], replicated, may hold values from 0 to 63, as said below
- far_mid_count: int32 [64], replicated, may hold values from 16 to 32
- far_top: int32 [8, 6], replicated, may hold values from 0 to 7, as said below
- far_top_count: int32 [8], replicated, may hold values from 1 to 6
Outputs:
- field: float32 [512, 4, 512], P('leaf')
The draws below stay inside these ranges and needn't reach their ends.
Inputs may be any that keep to these rules, and one draw needn't show every extreme that they name: `near_list`: slot 0 of leaf l's list is l itself; the slots of a list are distinct; with 16 leaves a device in Morton order, every entry of a leaf held by device d names a leaf of device d, one of the last 8 leaves of device d - 1 or one of the first 8 leaves of device d + 1. `far_mid`: the slots of a row are distinct nodes other than the row's own node. `far_top`: the slots of a row are distinct nodes other than the row's own node.
All inputs are finite; a program needn't handle non-finite values.
Results may differ from the reference program's by a relative error of at most 0.0003.
Values sent between devices are 32-bit elements; how exact they have to be, the bound alone decides.
A program may use at most 64 MiB of HBM per device.

```python
import jax
import jax.numpy as jnp
from jax import lax

LEAF = 512
RANK = 64
NRHS = 4
NEAR = 4
EDGE = 8
FAR1 = 32
FAR2 = 6
LEAVES_DEV = 16
NLEAF = 512
NP1 = 64
NP2 = 8


def draw_near_list(key, part):
    leaf_ids = jnp.arange(NLEAF)
    owner = leaf_ids // LEAVES_DEV
    span_width = LEAVES_DEV + 2 * EDGE
    slot_ids = jnp.arange(span_width)[None, :]
    candidates = owner[:, None] * LEAVES_DEV - EDGE + slot_ids
    usable = (candidates >= 0) & (candidates < NLEAF) & (candidates != leaf_ids[:, None])
    scores = jax.random.randint(key, (NLEAF, span_width), 0, 1 << 16) * span_width + slot_ids
    scores = jnp.where(usable, scores, (1 << 16) * span_width + slot_ids)
    order = jnp.argsort(scores, axis=1)[:, :NEAR - 1]
    others = jnp.take_along_axis(candidates, order, axis=1)
    return jnp.concatenate([leaf_ids[:, None], others], axis=1).astype(jnp.int32)


def pick_far(key, nodes, slots):
    keys = jax.random.split(key, nodes)
    shuffled = jax.vmap(lambda sub_key: jax.random.permutation(sub_key, nodes - 1))(keys)[:, :slots]
    target_ids = jnp.arange(nodes)[:, None]
    return jnp.where(shuffled >= target_ids, shuffled + 1, shuffled).astype(jnp.int32)


def draw_far_mid(key, part):
    return pick_far(jax.random.fold_in(key, 11), NP1, FAR1)


def draw_far_top(key, part):
    return pick_far(jax.random.fold_in(key, 23), NP2, FAR2)


def place_ends(result, key, least, largest):
    index_at = [jax.random.randint(jax.random.fold_in(key, axis), (), 0, length) for axis, length in enumerate(result.shape)]
    main_axis = result.shape.index(max(result.shape))
    beside = index_at[:main_axis] + [(index_at[main_axis] + 1) % result.shape[main_axis]] + index_at[main_axis + 1:]
    return result.at[tuple(index_at)].set(least).at[tuple(beside)].set(largest)


def block_levels(stream_key, extent, cuts, low, top_value):
    def one(dim, blocks):
        steps = jax.random.uniform(jax.random.fold_in(jax.random.fold_in(stream_key, 6), dim), (blocks,), jnp.float32, low / len(cuts), top_value / len(cuts))
        return jnp.repeat(jnp.exp(steps), extent[dim] // blocks).reshape((-1,) + (1,) * (len(extent) - dim - 1))

    factor_of = one(*cuts[0])
    for cut in cuts[1:]:
        factor_of = factor_of * one(*cut)
    return factor_of


def scatter_about(key, shape, deviation, limit, pieces=(), dtype=jnp.bfloat16):
    loudness = block_levels(key, shape, pieces, -0.22, 0.18) if pieces else 1.0
    values = jax.random.normal(key, shape, jnp.float32) * deviation * loudness
    return jnp.minimum(jnp.maximum(values, -limit), limit).astype(dtype)


def setup_inputs(seed: int = 0) -> dict:
    splits = jax.random.split(jax.random.key(seed), 14)
    coords = jnp.clip(1.0 * jax.random.uniform(splits[0], (NLEAF, 3, LEAF), jnp.float32) ** block_levels(splits[0], (NLEAF, 3, LEAF), ((0, 32),), -0.2, 0.2), 0.0, 1.0)
    charges = scatter_about(splits[1], (NLEAF, NRHS, LEAF), 1.0, 6.0, ((0, 32),), jnp.float32)
    bases = scatter_about(splits[2], (NLEAF, RANK, LEAF), LEAF ** -0.5, 0.25, ((0, 32),), jnp.float32)
    up_transfer = scatter_about(splits[3], (NLEAF, RANK, RANK), (8 * RANK) ** -0.5, 0.25, ((0, 32),), jnp.float32)
    top_transfer = scatter_about(splits[4], (NP1, RANK, RANK), RANK ** -0.5, 0.75, ((0, 32),), jnp.float32)
    proxy_mid = jnp.clip(jax.random.uniform(splits[5], (NP1, 3, RANK), jnp.float32, 0.0, 1.0), 0.0, 1.0)
    proxy_top = jnp.clip(jax.random.uniform(splits[6], (NP2, 3, RANK), jnp.float32, 0.0, 1.0), 0.0, 1.0)
    near_list = draw_near_list(jax.random.fold_in(splits[13], 71), 0)
    near_count = place_ends(jax.random.randint(splits[8], (NLEAF,), 1, NEAR + 1), jax.random.fold_in(splits[8], 1), 1, NEAR).astype(jnp.int32)
    far_mid = draw_far_mid(jax.random.fold_in(splits[13], 71), 0)
    far_mid_count = place_ends(jax.random.randint(splits[10], (NP1,), FAR1 // 2, FAR1 + 1), jax.random.fold_in(splits[10], 1), FAR1 // 2, FAR1).astype(jnp.int32)
    far_top = draw_far_top(jax.random.fold_in(splits[13], 71), 0)
    far_top_count = place_ends(jax.random.randint(splits[12], (NP2,), 1, FAR2 + 1), jax.random.fold_in(splits[12], 1), 1, FAR2).astype(jnp.int32)
    return {"coords": coords, "charges": charges, "bases": bases, "up_transfer": up_transfer, "top_transfer": top_transfer, "proxy_mid": proxy_mid, "proxy_top": proxy_top, "near_list": near_list, "near_count": near_count, "far_mid": far_mid, "far_mid_count": far_mid_count, "far_top": far_top, "far_top_count": far_top_count}


length_scale = 0.4
out_scale = 0.125
precise = lax.Precision.HIGHEST

def kernel(target_pts, source_pts):
    offset = target_pts[:, :, None] - source_pts[:, None, :]
    return jnp.exp(-jnp.sqrt(lax.optimization_barrier(jnp.sum(offset * offset, axis=0))) / length_scale)

def couple(target_proxy, source_proxy, coeffs, source_lists, counts):

    def single_target(packed_args):
        target_pts, source_ids, live_count = packed_args
        kernels = jax.vmap(kernel, (None, 0))(target_pts, source_proxy[source_ids])
        live_mask = (jnp.arange(source_ids.shape[0]) < live_count).astype(jnp.float32)
        return jnp.einsum('jab,jbk->ak', kernels * live_mask[:, None, None], coeffs[source_ids], precision=precise)
    return lax.map(single_target, (target_proxy, source_lists, counts))

def reference(coords, charges, bases, up_transfer, top_transfer, proxy_mid, proxy_top, near_list, near_count, far_mid, far_mid_count, far_top, far_top_count):
    leaf_coeffs = jnp.einsum('lrp,lkp->lrk', bases, charges, precision=precise)
    lifted_leaf = jnp.einsum('lrs,lsk->lrk', up_transfer, leaf_coeffs, precision=precise)
    mid_coeffs = lifted_leaf.reshape(NP1, 8, RANK, NRHS).sum(1)
    lifted_mid = jnp.einsum('nrs,nsk->nrk', top_transfer, mid_coeffs, precision=precise)
    top_coeffs = lifted_mid.reshape(NP2, 8, RANK, NRHS).sum(1)
    top_field = couple(proxy_top, proxy_top, top_coeffs, far_top, far_top_count)
    mid_far = couple(proxy_mid, proxy_mid, mid_coeffs, far_mid, far_mid_count)
    mid_field = mid_far + jnp.einsum('nsr,nsk->nrk', top_transfer, jnp.repeat(top_field, 8, axis=0), precision=precise)
    leaf_field = jnp.einsum('nsr,nsk->nrk', up_transfer, jnp.repeat(mid_field, 8, axis=0), precision=precise)
    far_part = jnp.einsum('lrp,lrk->lkp', bases, leaf_field, precision=precise)

    def near_leaf(packed_args):
        target_pts, source_ids, live_count = packed_args
        blocks = jax.vmap(kernel, (None, 0))(target_pts, coords[source_ids])
        live_mask = (jnp.arange(source_ids.shape[0]) < live_count).astype(jnp.float32)
        source_vals = charges[source_ids] * live_mask[:, None, None]
        return jnp.einsum('jts,jks->kt', blocks, source_vals, precision=precise)
    near_part = lax.map(near_leaf, (coords, near_list, near_count))
    return (near_part + far_part) * out_scale
```

```python
import functools

import jax
import jax.numpy as jnp
from jax import lax
from jax.experimental import pallas as pl
from jax.experimental.pallas import tpu as pltpu
from jax.sharding import PartitionSpec as P

EDGE = 8
FAN = 8
length_scale = 0.4
out_scale = 0.125
MESH = pl.DeviceIdType.MESH
TINY = 1e-30
UNIT = 1.4426950408889634 / length_scale
ROWS = 48
f32, bf16 = jnp.float32, jnp.bfloat16
NT = (((1,), (1,)), ((), ()))
NN = (((1,), (0,)), ((), ()))


def mm16(a, b, dims=NN):
    return lax.dot_general(a, b, dims, preferred_element_type=f32)


def halves(x):
    hi = x.astype(bf16)
    return hi, (x - hi.astype(f32)).astype(bf16)


def stacked(x):
    hi = x.astype(bf16).astype(f32)
    return jnp.concatenate([hi, x - hi], axis=0).astype(bf16)


def mm(a, b, dims=NN):
    bh, bl = halves(b)
    return folded(mm16(stacked(a), bh, dims)) + mm16(a.astype(bf16), bl, dims)


def folded(x):
    rows = x.shape[0] // 2
    return x[:rows] + x[rows:]


def decay(x):
    x = jnp.maximum(x, TINY)
    return jnp.exp2(-(x * lax.rsqrt(x)))


def weights(cols, rows):
    dx, dy, dz = (c - r for c, r in zip(cols, rows))
    return decay(dx * dx + dy * dy + dz * dz)


def columns_of(pts):
    pad = jnp.zeros((8 - pts.shape[0], pts.shape[1]), f32)
    return jnp.concatenate([pts, pad], axis=0).T


def rounded(x):
    return x.astype(bf16).astype(f32)


def pieces(x, count):
    out = []
    for _ in range(count):
        out.append(rounded(x))
        x = x - out[-1]
    return out


def factors(pts):
    points = pts.shape[1]
    zero = jnp.zeros((1, points), f32)
    at = lax.broadcasted_iota(jnp.int32, (8, points), 0)
    u = jnp.concatenate([pts, zero, pts, zero], axis=0)
    u = jnp.where((at & 3) < 3, (u - 0.5) * UNIT, 0.0)
    hi = jnp.floor(u * 64.0 + 0.5) * (1.0 / 64.0)
    r1, r2 = pieces(u - hi, 2)
    rest = r1 + r2
    upper = at < 4
    norm = jnp.sum(jnp.where(upper, hi * hi, 0.0), axis=0, keepdims=True)
    cross = jnp.sum(jnp.where(upper, (hi + hi + rest) * rest, 0.0), axis=0, keepdims=True)
    n1, n2 = pieces(norm, 2)
    a1, a2, a3 = pieces(cross, 3)

    ones = jnp.where(at < 7, 1.0, 0.0)
    low, six = jnp.where(at < 3, 1.0, 0.0), jnp.where(at < 6, 1.0, 0.0)
    crosses = jnp.where(at % 3 == 0, a1, jnp.where(at % 3 == 1, a2, a3))
    hi2, s1, s2 = -2.0 * hi, -2.0 * r1, -2.0 * r2
    source = [
        jnp.where(at < 3, hi, jnp.where(at == 3, n1, jnp.where(at == 4, n2, ones))),
        hi,
        r1,
        jnp.where(upper, r1, r2),
        r2,
        jnp.where(at < 3, crosses, six),
    ]
    target = [
        jnp.where(at < 3, hi2, jnp.where(at == 5, n1, jnp.where(at == 6, n2, ones))),
        jnp.where(upper, s1, s2),
        jnp.where(upper, hi2, s1),
        jnp.where(upper, s2, hi2),
        jnp.where(upper, s1, s2),
        jnp.where((at >= 3) & (at < 6), crosses, low),
    ]
    return source, target


def source_rows(parts):
    return jnp.concatenate(parts, axis=0).astype(bf16).T


def target_rows(parts):
    return jnp.concatenate(parts, axis=0).astype(bf16)


def run_blocks(blocks):
    steps = [(blk, i) for blk in blocks for i in range(len(blk[0]))]
    ahead = steps[0][0][1](*steps[0][0][0][0])
    for n, ((chunks, dist, kh_ref, kl_ref, beside), i) in enumerate(steps):
        now = ahead
        if n + 1 < len(steps):
            blk, k = steps[n + 1]
            ahead = blk[1](*blk[0][k])
        if i in beside:
            beside[i]()
        start, stop, lo, hi = chunks[i]
        kh, kl = halves(decay(now))
        kh_ref[start:stop, lo:hi] = kh
        kl_ref[start:stop, lo:hi] = kl


def distances(src_ref, tgt):
    return lambda start, stop, lo, hi: mm16(src_ref[start:stop, :], tgt[:, lo:hi])


def up_kernel(
    n,
    coords,
    charges,
    bases_hbm,
    up_hbm,
    top_hbm,
    before_c,
    before_q,
    after_c,
    after_q,
    gathered,
    own,
    targets,
    bases,
    up,
    top,
    load_sem,
    msg,
    src_a,
    src_b,
    kh_a,
    kl_a,
    kh_b,
    kl_b,
    send_sem,
    recv_sem,
    halo_send,
    halo_recv,
    own_sem,
):
    me = lax.axis_index("leaf")
    _, leaves, points = coords.shape
    ranks = bases.shape[1]
    nodes = top.shape[0]
    vectors = charges.shape[1]
    barrier = pltpu.get_barrier_semaphore()

    def greet(o, _):
        pl.semaphore_signal(
            barrier, inc=1, device_id=(lax.rem(me + o, n),), device_id_type=MESH
        )
        return 0

    lax.fori_loop(1, n, greet, 0)
    loads = [
        pltpu.make_async_copy(src, dst, load_sem.at[i])
        for i, (src, dst) in enumerate(((bases_hbm, bases), (up_hbm, up), (top_hbm, top)))
    ]
    for load in loads:
        load.start()

    def halo(i, src, dst, to):
        return pltpu.make_async_remote_copy(
            src_ref=src,
            dst_ref=dst,
            send_sem=halo_send.at[i],
            recv_sem=halo_recv.at[i],
            device_id=(to,),
            device_id_type=MESH,
        )

    nxt, prv = lax.rem(me + 1, n), lax.rem(me + n - 1, n)
    tail, head = pl.ds(leaves - EDGE, EDGE), pl.ds(0, EDGE)
    ups = [
        halo(0, coords.at[:, tail], before_c, nxt),
        halo(1, charges.at[tail], before_q, nxt),
    ]
    downs = [
        halo(2, coords.at[:, head], after_c, prv),
        halo(3, charges.at[head], after_q, prv),
    ]

    for load in loads:
        load.wait()
    msg[...] = jnp.zeros_like(msg)
    coeffs = [mm(charges[leaf], bases[leaf], NT) for leaf in range(leaves)]
    raised = [mm(coeffs[leaf], up[leaf], NT) for leaf in range(leaves)]
    mids = [functools.reduce(jnp.add, raised[p * FAN : (p + 1) * FAN]) for p in range(nodes)]
    lift = functools.reduce(jnp.add, [mm(mids[p], top[p], NT) for p in range(nodes)])
    for p in range(nodes):
        msg[0:vectors, p * ranks : (p + 1) * ranks] = mids[p]
    msg[vectors : 2 * vectors, 0:ranks] = lift
    pl.semaphore_wait(barrier, n - 1)

    @pl.when(me < n - 1)
    def _():
        for copy in ups:
            copy.start()

    @pl.when(me > 0)
    def _():
        for copy in downs:
            copy.start()

    half = points // 2
    last = leaves - 1

    def prepare(src, leaf):
        source, target = factors(coords[:, leaf])
        src[...] = source_rows(source)
        targets[leaf] = target_rows(target)

    chunks = [(c, c + 64, 0, points) for c in range(0, half, 64)]
    chunks += [(c, c + 128, half, points) for c in range(half, points, 128)]

    def product(kh_ref, kl_ref, leaf):
        q2 = stacked(charges[leaf])
        q_lo, q_hi = q2[:, :half], q2[:, half:]
        lo = hi = None
        for ref in (kh_ref, kl_ref):
            cross = ref[:half, half:]
            a = mm16(q_lo, ref[:half, :half]) + mm16(q_hi, cross, NT)
            b = mm16(q_lo, cross) + mm16(q_hi, ref[half:, half:])
            lo, hi = (a, b) if lo is None else (lo + a, hi + b)
        own[leaf, :, :half] = folded(lo)
        own[leaf, :, half:] = folded(hi)

    kh_b[...] = jnp.zeros_like(kh_b)
    kl_b[...] = jnp.zeros_like(kl_b)
    prepare(src_a, 0)

    def spread(to, slot):
        return pltpu.make_async_remote_copy(
            src_ref=msg,
            dst_ref=gathered.at[slot],
            send_sem=send_sem,
            recv_sem=recv_sem,
            device_id=(to,),
            device_id_type=MESH,
        )

    def send(o, _):
        spread(lax.rem(me + o, n), me).start()
        return 0

    lax.fori_loop(1, n, send, 0)
    mine = pltpu.make_async_copy(msg, gathered.at[me], own_sem)
    mine.start()

    def self_pair(i, _):
        leaf = 2 * i
        first = {
            1: lambda: product(kh_b, kl_b, jnp.maximum(leaf - 1, 0)),
            0: lambda: prepare(src_b, leaf + 1),
        }
        second = {
            1: lambda: product(kh_a, kl_a, leaf),
            0: lambda: prepare(src_a, jnp.minimum(leaf + 2, last)),
        }
        run_blocks(
            [
                (chunks, distances(src_a, targets[leaf]), kh_a, kl_a, first),
                (chunks, lambda *c: distances(src_b, targets[leaf + 1])(*c), kh_b, kl_b, second),
            ]
        )
        return 0

    lax.fori_loop(0, leaves // 2, self_pair, 0)
    product(kh_b, kl_b, last)
    mine.wait()

    others = gathered.at[pl.ds(0, n - 1)]
    for sem in (send_sem, recv_sem):
        pltpu.make_async_copy(others, others, sem).wait()

    @pl.when(me < n - 1)
    def _():
        for copy in ups:
            copy.wait_send()
        for copy in downs:
            copy.wait_recv()

    @pl.when(me > 0)
    def _():
        for copy in ups:
            copy.wait_recv()
        for copy in downs:
            copy.wait_send()


def down_kernel(
    near_list,
    near_count,
    far_mid,
    far_mid_count,
    far_top,
    far_top_count,
    coords,
    charges,
    before_c,
    before_q,
    after_c,
    after_q,
    gathered,
    targets,
    top,
    proxy_mid,
    proxy_top,
    own_hbm,
    up_hbm,
    bases_hbm,
    out,
    own,
    up,
    bases,
    src_a,
    src_b,
    kh_a,
    kl_a,
    kh_b,
    kl_b,
    acc,
    pair_leaf,
    pair_source,
    win_c,
    win_q,
    mid_t,
    src_pts,
    src_q,
    bases_sem,
):
    me = lax.axis_index("leaf")
    _, leaves, points = coords.shape
    ranks = bases.shape[1]
    nodes = top.shape[0]
    vectors = charges.shape[1]
    slots = far_mid.shape[0]
    top_slots = far_top.shape[1]
    fetches = [
        pltpu.make_async_copy(src, dst, bases_sem.at[i])
        for i, (src, dst) in enumerate(((bases_hbm, bases), (up_hbm, up), (own_hbm, own)))
    ]
    for fetch in fetches:
        fetch.start()
    win_c[:, 0:EDGE] = before_c[...]
    win_c[:, EDGE : EDGE + leaves] = coords[...]
    window = leaves + 2 * EDGE
    win_c[:, EDGE + leaves : window] = after_c[...]
    win_c[:, window:] = jnp.zeros_like(win_c[:, window:])
    win_q[0:EDGE] = before_q[...]
    win_q[EDGE : EDGE + leaves] = charges[...]
    win_q[EDGE + leaves : window] = after_q[...]
    win_q[window] = jnp.zeros_like(win_q[window])

    def coupled(target, live_slots, point_of, coeff_of, live):
        for j in range(live_slots):
            at = slice(j * ranks, (j + 1) * ranks)
            src_pts[0:3, at] = point_of(j) * UNIT
            src_q[:, at] = jnp.where(j < live, coeff_of(j), 0.0)
        cols = columns_of(target * UNIT)
        wide = live_slots * ranks
        total = jnp.zeros((2 * vectors, ranks), f32)
        step = min(512, wide)
        for lo in range(0, wide, step):
            at = slice(lo, min(lo + step, wide))
            k = weights([cols[:, i : i + 1] for i in range(3)], [src_pts[i : i + 1, at] for i in range(3)])
            kh, kl = halves(k)
            q2 = stacked(src_q[:, at])
            total = total + mm16(q2, kh, NT) + mm16(q2, kl, NT)
        return folded(total)

    per_top = FAN // nodes
    parent = (me * nodes) // FAN

    def top_coeff(j):
        s = far_top[parent, j]
        parts = [gathered[s * per_top + i, vectors : 2 * vectors, 0:ranks] for i in range(per_top)]
        return functools.reduce(jnp.add, parts)

    top_field = coupled(
        proxy_top[:, parent],
        top_slots,
        lambda j: proxy_top[:, far_top[parent, j]],
        top_coeff,
        far_top_count[parent],
    )
    for p in range(nodes):
        node = me * nodes + p

        def mid_coeff(j):
            s = far_mid[j, node]
            both = gathered[s // nodes, 0:vectors]
            out = both[:, 0:ranks]
            for i in range(1, nodes):
                out = jnp.where(s % nodes == i, both[:, i * ranks : (i + 1) * ranks], out)
            return out

        far = coupled(
            proxy_mid[:, node],
            slots,
            lambda j: proxy_mid[:, far_mid[j, node]],
            mid_coeff,
            far_mid_count[node],
        )
        mid_t[p] = far + mm(top_field, top[p])
    first = me * leaves - EDGE
    acc[...] = jnp.zeros_like(acc)
    kh_b[...] = jnp.zeros_like(kh_b)
    kl_b[...] = jnp.zeros_like(kl_b)
    pair_leaf[0] = 0
    pair_source[0] = window

    def enlist(leaf, at):
        for j in range(1, near_list.shape[0]):
            pair_leaf[at] = leaf
            pair_source[at] = near_list[j, leaf] - first
            at = at + (j < near_count[leaf]).astype(jnp.int32)
        return at

    total = lax.fori_loop(0, leaves, enlist, 1)
    for i in range(4):
        pair_leaf[total + i] = 0
        pair_source[total + i] = window

    def prepare(src, i):
        src[...] = source_rows(factors(win_c[:, pair_source[i]])[0])

    half = points // 2
    chunks = [(c, c + 64, 0, points) for c in range(0, points, 64)]

    def product(kh_ref, kl_ref, i, rows):
        q2 = stacked(win_q[pair_source[i]])[:, rows]
        acc[pair_leaf[i]] += mm16(q2, kh_ref[rows]) + mm16(q2, kl_ref[rows])

    def products(kh_ref, kl_ref, i):
        return {
            1: lambda: product(kh_ref, kl_ref, i, slice(0, half)),
            3: lambda: product(kh_ref, kl_ref, i, slice(half, points)),
        }

    prepare(src_a, 1)

    def pair(i, _):
        at = 2 * i + 1
        tgt_a, tgt_b = targets[pair_leaf[at]], targets[pair_leaf[at + 1]]
        first = {**products(kh_b, kl_b, at - 1), 0: lambda: prepare(src_b, at + 1)}
        second = {**products(kh_a, kl_a, at), 0: lambda: prepare(src_a, at + 2)}
        run_blocks(
            [
                (chunks, distances(src_a, tgt_a), kh_a, kl_a, first),
                (chunks, distances(src_b, tgt_b), kh_b, kl_b, second),
            ]
        )
        return 0

    trips = total // 2
    lax.fori_loop(0, trips, pair, 0)
    product(kh_b, kl_b, 2 * trips, slice(0, points))
    for fetch in fetches:
        fetch.wait()

    fields = [mm(mid_t[leaf // FAN], up[leaf]) for leaf in range(leaves)]
    for leaf in range(leaves):
        out[leaf] = (own[leaf] + folded(acc[leaf]) + mm(fields[leaf], bases[leaf])) * out_scale


def shards(
    coords,
    charges,
    bases,
    up_transfer,
    top_transfer,
    proxy_mid,
    proxy_top,
    near_list,
    near_count,
    far_mid,
    far_mid_count,
    far_top,
    far_top_count,
):
    n = lax.axis_size("leaf")
    leaves, vectors, points = charges.shape
    ranks = bases.shape[1]
    nodes = top_transfer.shape[0]
    vmem = pl.BlockSpec(memory_space=pltpu.VMEM)
    smem = pl.BlockSpec(memory_space=pltpu.SMEM)
    anywhere = pl.BlockSpec(memory_space=pl.ANY)
    like = jax.ShapeDtypeStruct
    coords, proxy_mid, proxy_top = (x.transpose(1, 0, 2) for x in (coords, proxy_mid, proxy_top))
    near_list, far_mid = near_list.T, far_mid.T
    edge_c, edge_q = like((3, EDGE, points), f32), like((EDGE, vectors, points), f32)
    *edges, gathered, own, targets = pl.pallas_call(
        functools.partial(up_kernel, n),
        out_shape=[
            edge_c,
            edge_q,
            edge_c,
            edge_q,
            like((n, 2 * vectors, nodes * ranks), f32),
            like((leaves, vectors, points), f32),
            like((leaves, ROWS, points), bf16),
        ],
        in_specs=[vmem] * 2 + [anywhere] * 3,
        out_specs=[anywhere] * 5 + [vmem] * 2,
        scratch_shapes=[
            pltpu.VMEM(bases.shape, f32),
            pltpu.VMEM(up_transfer.shape, f32),
            pltpu.VMEM(top_transfer.shape, f32),
            pltpu.SemaphoreType.DMA((3,)),
            pltpu.VMEM((2 * vectors, nodes * ranks), f32),
            pltpu.VMEM((points, ROWS), bf16),
            pltpu.VMEM((points, ROWS), bf16),
            pltpu.VMEM((points, points), bf16),
            pltpu.VMEM((points, points), bf16),
            pltpu.VMEM((points, points), bf16),
            pltpu.VMEM((points, points), bf16),
            pltpu.SemaphoreType.DMA,
            pltpu.SemaphoreType.DMA,
            pltpu.SemaphoreType.DMA((4,)),
            pltpu.SemaphoreType.DMA((4,)),
            pltpu.SemaphoreType.DMA,
        ],
        compiler_params=pltpu.CompilerParams(collective_id=0, has_side_effects=True),
        name="upward",
    )(coords, charges, bases, up_transfer, top_transfer)
    window = leaves + 2 * EDGE
    return pl.pallas_call(
        down_kernel,
        out_shape=like((leaves, vectors, points), f32),
        in_specs=[smem] * 6 + [vmem] * 11 + [anywhere] * 3,
        out_specs=vmem,
        scratch_shapes=[
            pltpu.VMEM((leaves, vectors, points), f32),
            pltpu.VMEM(up_transfer.shape, f32),
            pltpu.VMEM((leaves, ranks, points), f32),
            pltpu.VMEM((points, ROWS), bf16),
            pltpu.VMEM((points, ROWS), bf16),
            pltpu.VMEM((points, points), bf16),
            pltpu.VMEM((points, points), bf16),
            pltpu.VMEM((points, points), bf16),
            pltpu.VMEM((points, points), bf16),
            pltpu.VMEM((leaves, 2 * vectors, points), f32),
            pltpu.SMEM((leaves * (near_list.shape[0] - 1) + 4,), jnp.int32),
            pltpu.SMEM((leaves * (near_list.shape[0] - 1) + 4,), jnp.int32),
            pltpu.VMEM((3, window + 8, points), f32),
            pltpu.VMEM((window + 1, vectors, points), f32),
            pltpu.VMEM((nodes, vectors, ranks), f32),
            pltpu.VMEM((8, far_mid.shape[0] * ranks), f32),
            pltpu.VMEM((vectors, far_mid.shape[0] * ranks), f32),
            pltpu.SemaphoreType.DMA((3,)),
        ],
        name="downward",
    )(
        near_list,
        near_count,
        far_mid,
        far_mid_count,
        far_top,
        far_top_count,
        coords,
        charges,
        *edges,
        gathered,
        targets,
        top_transfer,
        proxy_mid,
        proxy_top,
        own,
        up_transfer,
        bases,
    )


def solution(mesh):
    placed = (
        P("leaf", None, None),
        P("leaf", None, None),
        P("leaf", None, None),
        P("leaf", None, None),
        P("leaf", None, None),
        P(),
        P(),
        P("leaf", None),
        P("leaf"),
        P(),
        P(),
        P(),
        P(),
    )
    return jax.shard_map(
        shards, mesh=mesh, in_specs=placed, out_specs=P("leaf", None, None), check_vma=False
    )
```

```python
import functools

import jax
import jax.numpy as jnp
from jax import lax
from jax.experimental import pallas as pl
from jax.experimental.pallas import tpu as pltpu
from jax.sharding import PartitionSpec as P

EDGE = 8
FAN = 8
length_scale = 0.4
out_scale = 0.125
MESH = pl.DeviceIdType.MESH
TINY = 1e-30
UNIT = 1.4426950408889634 / length_scale
ROWS = 32
AHEAD = 3
f32, bf16 = jnp.float32, jnp.bfloat16
NT = (((1,), (1,)), ((), ()))
NN = (((1,), (0,)), ((), ()))


def mm16(a, b, dims=NN):
    return lax.dot_general(a, b, dims, preferred_element_type=f32)


def halves(x):
    hi = x.astype(bf16)
    return hi, (x - hi.astype(f32)).astype(bf16)


def stacked(x):
    hi = x.astype(bf16).astype(f32)
    return jnp.concatenate([hi, x - hi], axis=0).astype(bf16)


def mm(a, b, dims=NN):
    bh, bl = halves(b)
    return folded(mm16(stacked(a), bh, dims)) + mm16(a.astype(bf16), bl, dims)


def folded(x):
    rows = x.shape[0] // 2
    return x[:rows] + x[rows:]


def decay(x):
    return jnp.exp2(-(x * lax.rsqrt(x)))


def weights(cols, rows):
    dx, dy, dz = (c - r for c, r in zip(cols, rows))
    return decay(jnp.maximum(dx * dx + dy * dy + dz * dz, TINY))


def columns_of(pts):
    pad = jnp.zeros((8 - pts.shape[0], pts.shape[1]), f32)
    return jnp.concatenate([pts, pad], axis=0).T


def rounded(x):
    return x.astype(bf16).astype(f32)


def pieces(x, count):
    out = []
    for _ in range(count):
        out.append(rounded(x))
        x = x - out[-1]
    return out


def factors(pts):
    points = pts.shape[1]
    blank = jnp.full((1, points), 0.5, f32)
    at = lax.broadcasted_iota(jnp.int32, (8, points), 0)
    u = (jnp.concatenate([pts, blank, pts, blank], axis=0) - 0.5) * UNIT
    hi = jnp.floor(u * 64.0 + 0.5) * (1.0 / 64.0)
    rest = rounded(u - hi)
    upper = at < 4
    twice = hi + hi
    norm = jnp.sum(jnp.where(upper, hi * hi, 0.0), axis=0, keepdims=True)
    cross = jnp.sum(jnp.where(upper, (twice + rest) * rest, 0.0), axis=0, keepdims=True)
    n1, n2 = pieces(norm, 2)
    a1, a2, a3 = pieces(cross, 3)
    third, last = at == 3, at == 7
    fifth, five = at == 5, at < 5
    down = jnp.where(third | last, 1.0, jnp.where(upper, -twice, -2.0 * rest))
    source = [
        jnp.where(third, n1, jnp.where(last, n2, hi)),
        jnp.where(third, a1, jnp.where(last, a2, rest)),
        jnp.where(five, 1.0, jnp.where(fifth, a3, 0.0)),
        jnp.zeros_like(u),
    ]
    low = jnp.where(at == 2, a1, jnp.where(at == 3, a2, jnp.where(at == 4, a3, jnp.where(fifth, 1.0, 0.0))))
    target = [down, down, jnp.where(at == 0, n1, jnp.where(at == 1, n2, low)), jnp.zeros_like(u)]
    return source, target


def source_rows(parts):
    return jnp.concatenate(parts, axis=0).astype(bf16).T


def target_rows(parts):
    return jnp.concatenate(parts, axis=0).astype(bf16)


def measure(dst, src, tgt, chunk):
    start, stop, lo, hi = chunk
    dst[start:stop, lo:hi] = jnp.maximum(mm16(src[start:stop, :], tgt[:, lo:hi]), TINY)


def settle(x_ref, k_refs, chunk):
    start, stop, lo, hi = chunk
    kh, kl = halves(decay(x_ref[start:stop, lo:hi]))
    k_refs[0][start:stop, lo:hi] = kh
    k_refs[1][start:stop, lo:hi] = kl


def pipeline(chunks, ahead, fetch, xs, ks, beside):
    n = len(chunks)
    for j in range(2 * n):
        b, c = divmod(j + ahead, n)
        measure(xs[b % 2], *fetch[b], chunks[c])
        b, c = divmod(j, n)
        if (b, c) in beside:
            beside[b, c]()
        settle(xs[b], ks[b], chunks[c])


def up_kernel(
    n,
    coords,
    charges,
    bases_hbm,
    up_hbm,
    top_hbm,
    before_c,
    before_q,
    after_c,
    after_q,
    gathered,
    own,
    sources_hbm,
    targets_hbm,
    bases,
    up,
    top,
    load_sem,
    msg,
    sources,
    targets,
    x_a,
    x_b,
    kh_a,
    kl_a,
    kh_b,
    kl_b,
    send_sem,
    recv_sem,
    halo_send,
    halo_recv,
    own_sem,
):
    me = lax.axis_index("leaf")
    _, leaves, points = coords.shape
    ranks = bases.shape[1]
    nodes = top.shape[0]
    vectors = charges.shape[1]
    barrier = pltpu.get_barrier_semaphore()

    def greet(o, _):
        pl.semaphore_signal(
            barrier, inc=1, device_id=(lax.rem(me + o, n),), device_id_type=MESH
        )
        return 0

    lax.fori_loop(1, n, greet, 0)
    loads = [
        pltpu.make_async_copy(src, dst, load_sem.at[i])
        for i, (src, dst) in enumerate(((bases_hbm, bases), (up_hbm, up), (top_hbm, top)))
    ]
    for load in loads:
        load.start()

    def halo(i, src, dst, to):
        return pltpu.make_async_remote_copy(
            src_ref=src,
            dst_ref=dst,
            send_sem=halo_send.at[i],
            recv_sem=halo_recv.at[i],
            device_id=(to,),
            device_id_type=MESH,
        )

    nxt, prv = lax.rem(me + 1, n), lax.rem(me + n - 1, n)
    tail, head = pl.ds(leaves - EDGE, EDGE), pl.ds(0, EDGE)
    ups = [
        halo(0, coords.at[:, tail], before_c, nxt),
        halo(1, charges.at[tail], before_q, nxt),
    ]
    downs = [
        halo(2, coords.at[:, head], after_c, prv),
        halo(3, charges.at[head], after_q, prv),
    ]

    def prepare(i, _):
        for u in range(4):
            source, target = factors(coords[:, 4 * i + u])
            sources[4 * i + u] = source_rows(source)
            targets[4 * i + u] = target_rows(target)
        return 0

    lax.fori_loop(0, leaves // 4, prepare, 0)
    keeps = [
        pltpu.make_async_copy(src, dst, own_sem.at[1 + i])
        for i, (src, dst) in enumerate(((sources, sources_hbm), (targets, targets_hbm)))
    ]
    for keep in keeps:
        keep.start()
    msg[...] = jnp.zeros_like(msg)
    for load in loads:
        load.wait()
    coeffs = [mm(charges[leaf], bases[leaf], NT) for leaf in range(leaves)]
    raised = [mm(coeffs[leaf], up[leaf], NT) for leaf in range(leaves)]
    mids = [functools.reduce(jnp.add, raised[p * FAN : (p + 1) * FAN]) for p in range(nodes)]
    lift = functools.reduce(jnp.add, [mm(mids[p], top[p], NT) for p in range(nodes)])
    for p in range(nodes):
        msg[0:vectors, p * ranks : (p + 1) * ranks] = mids[p]
    msg[vectors : 2 * vectors, 0:ranks] = lift
    pl.semaphore_wait(barrier, n - 1)

    @pl.when(me < n - 1)
    def _():
        for copy in ups:
            copy.start()

    @pl.when(me > 0)
    def _():
        for copy in downs:
            copy.start()

    half = points // 2
    last = leaves - 1
    chunks = [(c, c + 64, 0, points) for c in range(0, half, 64)]
    chunks += [(c, c + 128, half, points) for c in range(half, points, 128)]
    xs, ks = (x_a, x_b), ((kh_a, kl_a), (kh_b, kl_b))

    def early(k_refs, leaf):
        q2 = stacked(charges[leaf])
        q_lo, q_hi = q2[:, :half], q2[:, half:]
        lo = hi = None
        for ref in k_refs:
            cross = ref[:half, half:]
            a = mm16(q_lo, ref[:half, :half]) + mm16(q_hi, cross, NT)
            b = mm16(q_lo, cross)
            lo, hi = (a, b) if lo is None else (lo + a, hi + b)
        own[leaf, :, :half] = folded(lo)
        own[leaf, :, half:] = folded(hi)

    def late(k_refs, leaf):
        q_hi = stacked(charges[leaf])[:, half:]
        hi = mm16(q_hi, k_refs[0][half:, half:]) + mm16(q_hi, k_refs[1][half:, half:])
        own[leaf, :, half:] += folded(hi)

    kh_b[...] = jnp.zeros_like(kh_b)
    kl_b[...] = jnp.zeros_like(kl_b)
    own[0] = jnp.zeros_like(own[0])
    for chunk in chunks[:AHEAD]:
        measure(x_a, sources.at[0], targets[0], chunk)

    def spread(to, slot):
        return pltpu.make_async_remote_copy(
            src_ref=msg,
            dst_ref=gathered.at[slot],
            send_sem=send_sem,
            recv_sem=recv_sem,
            device_id=(to,),
            device_id_type=MESH,
        )

    def send(o, _):
        spread(lax.rem(me + o, n), me).start()
        return 0

    lax.fori_loop(1, n, send, 0)
    mine = pltpu.make_async_copy(msg, gathered.at[me], own_sem.at[0])
    mine.start()

    def self_pair(i, _):
        leaf = 2 * i
        after = jnp.minimum(leaf + 2, last)
        fetch = [(sources.at[k], targets[k]) for k in (leaf, leaf + 1, after)]
        beside = {
            (0, 0): lambda: late(ks[1], jnp.maximum(leaf - 1, 0)),
            (0, 4): lambda: early(ks[0], leaf),
            (1, 0): lambda: late(ks[0], leaf),
            (1, 4): lambda: early(ks[1], leaf + 1),
        }
        pipeline(chunks, AHEAD, fetch, xs, ks, beside)
        return 0

    lax.fori_loop(0, leaves // 2, self_pair, 0)
    late(ks[1], last)
    for keep in keeps:
        keep.wait()
    mine.wait()

    others = gathered.at[pl.ds(0, n - 1)]
    for sem in (send_sem, recv_sem):
        pltpu.make_async_copy(others, others, sem).wait()

    @pl.when(me < n - 1)
    def _():
        for copy in ups:
            copy.wait_send()
        for copy in downs:
            copy.wait_recv()

    @pl.when(me > 0)
    def _():
        for copy in ups:
            copy.wait_recv()
        for copy in downs:
            copy.wait_send()


def down_kernel(
    near_list,
    near_count,
    far_mid,
    far_mid_count,
    far_top,
    far_top_count,
    coords,
    charges,
    before_c,
    before_q,
    after_c,
    after_q,
    gathered,
    top,
    proxy_mid,
    proxy_top,
    own_hbm,
    up_hbm,
    bases_hbm,
    sources_hbm,
    targets_hbm,
    out,
    own,
    up,
    bases,
    sources,
    targets,
    x_a,
    x_b,
    kh_a,
    kl_a,
    kh_b,
    kl_b,
    acc,
    pair_leaf,
    pair_source,
    win_q,
    mid_t,
    src_pts,
    src_q,
    bases_sem,
):
    me = lax.axis_index("leaf")
    _, leaves, points = coords.shape
    ranks = bases.shape[1]
    nodes = top.shape[0]
    vectors = charges.shape[1]
    slots = far_mid.shape[0]
    top_slots = far_top.shape[1]
    window = leaves + 2 * EDGE
    fetches = [
        pltpu.make_async_copy(src, dst, bases_sem.at[i])
        for i, (src, dst) in enumerate(
            (
                (sources_hbm, sources.at[pl.ds(EDGE, leaves)]),
                (targets_hbm, targets),
                (bases_hbm, bases),
                (up_hbm, up),
                (own_hbm, own),
            )
        )
    ]
    for fetch in fetches:
        fetch.start()

    def outside(i, _):
        for u in range(2):
            sources[2 * i + u] = source_rows(factors(before_c[:, 2 * i + u])[0])
            sources[EDGE + leaves + 2 * i + u] = source_rows(factors(after_c[:, 2 * i + u])[0])
        return 0

    lax.fori_loop(0, EDGE // 2, outside, 0)
    sources[window] = jnp.zeros_like(sources[window])
    win_q[0:EDGE] = before_q[...]
    win_q[EDGE : EDGE + leaves] = charges[...]
    win_q[EDGE + leaves : window] = after_q[...]
    win_q[window] = jnp.zeros_like(win_q[window])

    def coupled(target, live_slots, point_of, coeff_of, live):
        for j in range(live_slots):
            at = slice(j * ranks, (j + 1) * ranks)
            src_pts[0:3, at] = point_of(j) * UNIT
            src_q[:, at] = jnp.where(j < live, coeff_of(j), 0.0)
        cols = columns_of(target * UNIT)
        wide = live_slots * ranks
        total = jnp.zeros((2 * vectors, ranks), f32)
        step = min(512, wide)
        for lo in range(0, wide, step):
            at = slice(lo, min(lo + step, wide))
            k = weights([cols[:, i : i + 1] for i in range(3)], [src_pts[i : i + 1, at] for i in range(3)])
            kh, kl = halves(k)
            q2 = stacked(src_q[:, at])
            total = total + mm16(q2, kh, NT) + mm16(q2, kl, NT)
        return folded(total)

    per_top = FAN // nodes
    parent = (me * nodes) // FAN

    def top_coeff(j):
        s = far_top[parent, j]
        parts = [gathered[s * per_top + i, vectors : 2 * vectors, 0:ranks] for i in range(per_top)]
        return functools.reduce(jnp.add, parts)

    top_field = coupled(
        proxy_top[:, parent],
        top_slots,
        lambda j: proxy_top[:, far_top[parent, j]],
        top_coeff,
        far_top_count[parent],
    )
    for p in range(nodes):
        node = me * nodes + p

        def mid_coeff(j):
            s = far_mid[j, node]
            both = gathered[s // nodes, 0:vectors]
            out = both[:, 0:ranks]
            for i in range(1, nodes):
                out = jnp.where(s % nodes == i, both[:, i * ranks : (i + 1) * ranks], out)
            return out

        far = coupled(
            proxy_mid[:, node],
            slots,
            lambda j: proxy_mid[:, far_mid[j, node]],
            mid_coeff,
            far_mid_count[node],
        )
        mid_t[p] = far + mm(top_field, top[p])
    first = me * leaves - EDGE
    acc[...] = jnp.zeros_like(acc)
    kh_b[...] = jnp.zeros_like(kh_b)
    kl_b[...] = jnp.zeros_like(kl_b)
    pair_leaf[0] = 0
    pair_source[0] = window

    def enlist(leaf, at):
        for j in range(1, near_list.shape[0]):
            pair_leaf[at] = leaf
            pair_source[at] = near_list[j, leaf] - first
            at = at + (j < near_count[leaf]).astype(jnp.int32)
        return at

    total = lax.fori_loop(0, leaves, enlist, 1)
    for i in range(4):
        pair_leaf[total + i] = 0
        pair_source[total + i] = window

    half = points // 2
    chunks = [(c, c + 64, 0, points) for c in range(0, points, 64)]
    xs, ks = (x_a, x_b), ((kh_a, kl_a), (kh_b, kl_b))

    def product(k_refs, i, rows):
        q2 = stacked(win_q[pair_source[i]])[:, rows]
        acc[pair_leaf[i]] += mm16(q2, k_refs[0][rows]) + mm16(q2, k_refs[1][rows])

    top_rows, low_rows = slice(0, half), slice(half, points)
    for fetch in fetches[:2]:
        fetch.wait()
    for chunk in chunks[:AHEAD]:
        measure(x_a, sources.at[pair_source[1]], targets[pair_leaf[1]], chunk)

    def pair(i, _):
        at = 2 * i + 1
        fetch = [(sources.at[pair_source[k]], targets[pair_leaf[k]]) for k in (at, at + 1, at + 2)]
        beside = {
            (0, 0): lambda: product(ks[1], at - 1, low_rows),
            (0, 4): lambda: product(ks[0], at, top_rows),
            (1, 0): lambda: product(ks[0], at, low_rows),
            (1, 4): lambda: product(ks[1], at + 1, top_rows),
        }
        pipeline(chunks, AHEAD, fetch, xs, ks, beside)
        return 0

    trips = total // 2
    lax.fori_loop(0, trips, pair, 0)
    product(ks[1], 2 * trips, low_rows)
    for fetch in fetches[2:]:
        fetch.wait()
    fields = [mm(mid_t[leaf // FAN], up[leaf]) for leaf in range(leaves)]
    for leaf in range(leaves):
        out[leaf] = (own[leaf] + folded(acc[leaf]) + mm(fields[leaf], bases[leaf])) * out_scale


def shards(
    coords,
    charges,
    bases,
    up_transfer,
    top_transfer,
    proxy_mid,
    proxy_top,
    near_list,
    near_count,
    far_mid,
    far_mid_count,
    far_top,
    far_top_count,
):
    n = lax.axis_size("leaf")
    leaves, vectors, points = charges.shape
    ranks = bases.shape[1]
    nodes = top_transfer.shape[0]
    vmem = pl.BlockSpec(memory_space=pltpu.VMEM)
    smem = pl.BlockSpec(memory_space=pltpu.SMEM)
    anywhere = pl.BlockSpec(memory_space=pl.ANY)
    like = jax.ShapeDtypeStruct
    coords, proxy_mid, proxy_top = (x.transpose(1, 0, 2) for x in (coords, proxy_mid, proxy_top))
    near_list, far_mid = near_list.T, far_mid.T
    edge_c, edge_q = like((3, EDGE, points), f32), like((EDGE, vectors, points), f32)
    *edges, gathered, own, sources, targets = pl.pallas_call(
        functools.partial(up_kernel, n),
        out_shape=[
            edge_c,
            edge_q,
            edge_c,
            edge_q,
            like((n, 2 * vectors, nodes * ranks), f32),
            like((leaves, vectors, points), f32),
            like((leaves, points, ROWS), bf16),
            like((leaves, ROWS, points), bf16),
        ],
        in_specs=[vmem] * 2 + [anywhere] * 3,
        out_specs=[anywhere] * 5 + [vmem] + [anywhere] * 2,
        scratch_shapes=[
            pltpu.VMEM(bases.shape, f32),
            pltpu.VMEM(up_transfer.shape, f32),
            pltpu.VMEM(top_transfer.shape, f32),
            pltpu.SemaphoreType.DMA((3,)),
            pltpu.VMEM((2 * vectors, nodes * ranks), f32),
            pltpu.VMEM((leaves, points, ROWS), bf16),
            pltpu.VMEM((leaves, ROWS, points), bf16),
            pltpu.VMEM((points, points), f32),
            pltpu.VMEM((points, points), f32),
            pltpu.VMEM((points, points), bf16),
            pltpu.VMEM((points, points), bf16),
            pltpu.VMEM((points, points), bf16),
            pltpu.VMEM((points, points), bf16),
            pltpu.SemaphoreType.DMA,
            pltpu.SemaphoreType.DMA,
            pltpu.SemaphoreType.DMA((4,)),
            pltpu.SemaphoreType.DMA((4,)),
            pltpu.SemaphoreType.DMA((3,)),
        ],
        compiler_params=pltpu.CompilerParams(
            collective_id=0, has_side_effects=True, vmem_limit_bytes=60 << 20
        ),
        name="upward",
    )(coords, charges, bases, up_transfer, top_transfer)
    window = leaves + 2 * EDGE
    return pl.pallas_call(
        down_kernel,
        out_shape=like((leaves, vectors, points), f32),
        in_specs=[smem] * 6 + [vmem] * 10 + [anywhere] * 5,
        out_specs=vmem,
        scratch_shapes=[
            pltpu.VMEM((leaves, vectors, points), f32),
            pltpu.VMEM(up_transfer.shape, f32),
            pltpu.VMEM((leaves, ranks, points), f32),
            pltpu.VMEM((window + 1, points, ROWS), bf16),
            pltpu.VMEM((leaves, ROWS, points), bf16),
            pltpu.VMEM((points, points), f32),
            pltpu.VMEM((points, points), f32),
            pltpu.VMEM((points, points), bf16),
            pltpu.VMEM((points, points), bf16),
            pltpu.VMEM((points, points), bf16),
            pltpu.VMEM((points, points), bf16),
            pltpu.VMEM((leaves, 2 * vectors, points), f32),
            pltpu.SMEM((leaves * (near_list.shape[0] - 1) + 4,), jnp.int32),
            pltpu.SMEM((leaves * (near_list.shape[0] - 1) + 4,), jnp.int32),
            pltpu.VMEM((window + 1, vectors, points), f32),
            pltpu.VMEM((nodes, vectors, ranks), f32),
            pltpu.VMEM((8, far_mid.shape[0] * ranks), f32),
            pltpu.VMEM((vectors, far_mid.shape[0] * ranks), f32),
            pltpu.SemaphoreType.DMA((5,)),
        ],
        compiler_params=pltpu.CompilerParams(vmem_limit_bytes=60 << 20),
        name="downward",
    )(
        near_list,
        near_count,
        far_mid,
        far_mid_count,
        far_top,
        far_top_count,
        coords,
        charges,
        *edges,
        gathered,
        top_transfer,
        proxy_mid,
        proxy_top,
        own,
        up_transfer,
        bases,
        sources,
        targets,
    )


def solution(mesh):
    placed = (
        P("leaf", None, None),
        P("leaf", None, None),
        P("leaf", None, None),
        P("leaf", None, None),
        P("leaf", None, None),
        P(),
        P(),
        P("leaf", None),
        P("leaf"),
        P(),
        P(),
        P(),
        P(),
    )
    return jax.shard_map(
        shards, mesh=mesh, in_specs=placed, out_specs=P("leaf", None, None), check_vma=False
    )
```

```python
import functools

import jax
import jax.numpy as jnp
from jax import lax
from jax.experimental import pallas as pl
from jax.experimental.pallas import tpu as pltpu
from jax.sharding import PartitionSpec as P

EDGE = 8
FAN = 8
length_scale = 0.4
out_scale = 0.125
MESH = pl.DeviceIdType.MESH
TINY = 1e-30
UNIT = 1.4426950408889634 / length_scale
ROWS = 32
AHEAD = 3
AHEAD_UP = 2
f32, bf16 = jnp.float32, jnp.bfloat16
NT = (((1,), (1,)), ((), ()))
NN = (((1,), (0,)), ((), ()))


def mm16(a, b, dims=NN):
    return lax.dot_general(a, b, dims, preferred_element_type=f32)


def halves(x):
    hi = x.astype(bf16)
    return hi, (x - hi.astype(f32)).astype(bf16)


def stacked(x):
    hi = x.astype(bf16).astype(f32)
    return jnp.concatenate([hi, x - hi], axis=0).astype(bf16)


def mm(a, b, dims=NN):
    bh, bl = halves(b)
    return folded(mm16(stacked(a), bh, dims)) + mm16(a.astype(bf16), bl, dims)


def folded(x):
    rows = x.shape[0] // 2
    return x[:rows] + x[rows:]


def decay(x):
    return jnp.exp2(-(x * lax.rsqrt(x)))


def weights(cols, rows):
    dx, dy, dz = (c - r for c, r in zip(cols, rows))
    return decay(jnp.maximum(dx * dx + dy * dy + dz * dz, TINY))


def columns_of(pts):
    pad = jnp.zeros((8 - pts.shape[0], pts.shape[1]), f32)
    return jnp.concatenate([pts, pad], axis=0).T


def rounded(x):
    return x.astype(bf16).astype(f32)


def pieces(x, count):
    out = []
    for _ in range(count):
        out.append(rounded(x))
        x = x - out[-1]
    return out


def factors(pts):
    points = pts.shape[1]
    blank = jnp.full((1, points), 0.5, f32)
    at = lax.broadcasted_iota(jnp.int32, (8, points), 0)
    u = (jnp.concatenate([pts, blank, pts, blank], axis=0) - 0.5) * UNIT
    hi = jnp.floor(u * 64.0 + 0.5) * (1.0 / 64.0)
    rest = rounded(u - hi)
    upper = at < 4
    twice = hi + hi
    norm = jnp.sum(jnp.where(upper, hi * hi, 0.0), axis=0, keepdims=True)
    cross = jnp.sum(jnp.where(upper, (twice + rest) * rest, 0.0), axis=0, keepdims=True)
    n1, n2 = pieces(norm, 2)
    a1, a2, a3 = pieces(cross, 3)
    third, last = at == 3, at == 7
    fifth, five = at == 5, at < 5
    down = jnp.where(third | last, 1.0, jnp.where(upper, -twice, -2.0 * rest))
    source = [
        jnp.where(third, n1, jnp.where(last, n2, hi)),
        jnp.where(third, a1, jnp.where(last, a2, rest)),
        jnp.where(five, 1.0, jnp.where(fifth, a3, 0.0)),
        jnp.zeros_like(u),
    ]
    low = jnp.where(at == 2, a1, jnp.where(at == 3, a2, jnp.where(at == 4, a3, jnp.where(fifth, 1.0, 0.0))))
    target = [down, down, jnp.where(at == 0, n1, jnp.where(at == 1, n2, low)), jnp.zeros_like(u)]
    return source, target


def source_rows(parts):
    return jnp.concatenate(parts, axis=0).astype(bf16).T


def target_rows(parts):
    return jnp.concatenate(parts, axis=0).astype(bf16)


def measure(dst, src, tgt, chunk, clamp=True):
    start, stop, lo, hi = chunk
    x = mm16(src[start:stop, :], tgt[:, lo:hi])
    dst[start:stop, lo:hi] = jnp.maximum(x, TINY) if clamp else x


def settle(x_ref, k_refs, chunk):
    start, stop, lo, hi = chunk
    kh, kl = halves(decay(x_ref[start:stop, lo:hi]))
    k_refs[0][start:stop, lo:hi] = kh
    k_refs[1][start:stop, lo:hi] = kl


def pipeline(chunks, ahead, fetch, xs, ks, beside, clamp=True):
    n = len(chunks)
    for j in range(2 * n):
        b, c = divmod(j + ahead, n)
        measure(xs[b % 2], *fetch[b], chunks[c], clamp)
        b, c = divmod(j, n)
        if (b, c) in beside:
            beside[b, c]()
        settle(xs[b], ks[b], chunks[c])


def up_kernel(
    n,
    coords,
    charges,
    bases_hbm,
    up_hbm,
    top_hbm,
    before_c,
    before_q,
    after_c,
    after_q,
    gathered,
    own,
    sources_hbm,
    targets_hbm,
    bases,
    up,
    top,
    load_sem,
    msg,
    sources,
    targets,
    x_a,
    x_b,
    kh_a,
    kl_a,
    kh_b,
    kl_b,
    send_sem,
    recv_sem,
    halo_send,
    halo_recv,
    own_sem,
    pass_sem,
):
    me = lax.axis_index("leaf")
    _, leaves, points = coords.shape
    ranks = bases.shape[1]
    nodes = top.shape[0]
    vectors = charges.shape[1]
    barrier = pltpu.get_barrier_semaphore()

    chips = n // 2
    core, chip = lax.rem(me, 2), me // 2
    sibling = me + 1 - 2 * core
    outer = lax.rem(me + n - 1 + 2 * core, n)

    def peer(o):
        return 2 * lax.rem(chip + o, chips) + core

    def hail(to):
        pl.semaphore_signal(barrier, inc=1, device_id=(to,), device_id_type=MESH)

    def greet(o, _):
        hail(peer(o))
        return 0

    hail(sibling)
    hail(outer)
    lax.fori_loop(1, chips, greet, 0)
    loads = [
        pltpu.make_async_copy(src, dst, load_sem.at[i])
        for i, (src, dst) in enumerate(((bases_hbm, bases), (up_hbm, up), (top_hbm, top)))
    ]
    for load in loads:
        load.start()

    def halo(i, src, dst, to):
        return pltpu.make_async_remote_copy(
            src_ref=src,
            dst_ref=dst,
            send_sem=halo_send.at[i],
            recv_sem=halo_recv.at[i],
            device_id=(to,),
            device_id_type=MESH,
        )

    nxt, prv = lax.rem(me + 1, n), lax.rem(me + n - 1, n)
    tail, head = pl.ds(leaves - EDGE, EDGE), pl.ds(0, EDGE)
    ups = [
        halo(0, coords.at[:, tail], before_c, nxt),
        halo(1, charges.at[tail], before_q, nxt),
    ]
    downs = [
        halo(2, coords.at[:, head], after_c, prv),
        halo(3, charges.at[head], after_q, prv),
    ]

    def prepare(leaf):
        source, target = factors(coords[:, leaf])
        sources[leaf] = source_rows(source)
        targets[leaf] = target_rows(target)

    def prepare_some(i, _):
        for u in range(4):
            prepare(4 * i + u)
        return 0

    before = leaves // 2
    lax.fori_loop(0, before // 4, prepare_some, 0)
    msg[...] = jnp.zeros_like(msg)
    for load in loads:
        load.wait()
    for leaf in range(before, leaves):
        prepare(leaf)
    coeffs = [mm(charges[leaf], bases[leaf], NT) for leaf in range(leaves)]
    raised = [mm(coeffs[leaf], up[leaf], NT) for leaf in range(leaves)]
    mids = [functools.reduce(jnp.add, raised[p * FAN : (p + 1) * FAN]) for p in range(nodes)]
    lift = functools.reduce(jnp.add, [mm(mids[p], top[p], NT) for p in range(nodes)])
    for p in range(nodes):
        msg[0:vectors, p * ranks : (p + 1) * ranks] = mids[p]
    msg[vectors : 2 * vectors, 0:ranks] = lift
    keeps = [
        pltpu.make_async_copy(src, dst, own_sem.at[1 + i])
        for i, (src, dst) in enumerate(((sources, sources_hbm), (targets, targets_hbm)))
    ]
    for keep in keeps:
        keep.start()
    half = points // 2
    last = leaves - 1
    quarter = points // 4
    chunks = [(c, c + 64, c // quarter * quarter, points) for c in range(0, half, 64)]
    chunks += [(c, c + quarter, c, points) for c in range(half, points, quarter)]
    xs, ks = (x_a, x_b), ((kh_a, kl_a), (kh_b, kl_b))

    def mirror(k_refs, at):
        here, there = slice(at, at + quarter), slice(at + quarter, at + 2 * quarter)
        for ref in k_refs:
            ref[there, here] = ref[here, there].T

    def early(k_refs, leaf):
        q2 = stacked(charges[leaf])
        q_lo, q_hi = q2[:, :half], q2[:, half:]
        lo = hi = None
        for ref in k_refs:
            cross = ref[:half, half:]
            a = mm16(q_lo, ref[:half, :half]) + mm16(q_hi, cross, NT)
            b = mm16(q_lo, cross)
            lo, hi = (a, b) if lo is None else (lo + a, hi + b)
        own[leaf, :, :half] = folded(lo)
        own[leaf, :, half:] = folded(hi)

    def late(k_refs, leaf):
        q_hi = stacked(charges[leaf])[:, half:]
        hi = mm16(q_hi, k_refs[0][half:, half:]) + mm16(q_hi, k_refs[1][half:, half:])
        own[leaf, :, half:] += folded(hi)

    kh_b[...] = jnp.zeros_like(kh_b)
    kl_b[...] = jnp.zeros_like(kl_b)
    own[0] = jnp.zeros_like(own[0])
    for chunk in chunks[:AHEAD_UP]:
        measure(x_a, sources.at[0], targets[0], chunk)

    def send(o, _):
        pltpu.make_async_remote_copy(
            src_ref=msg,
            dst_ref=gathered.at[core, chip],
            send_sem=send_sem,
            recv_sem=recv_sem,
            device_id=(peer(o),),
            device_id_type=MESH,
        ).start()
        return 0

    pl.semaphore_wait(barrier, chips + 1)
    lax.fori_loop(1, chips, send, 0)
    mine = pltpu.make_async_copy(msg, gathered.at[core, chip], own_sem.at[0])
    mine.start()

    @pl.when(me < n - 1)
    def _():
        for copy in ups:
            copy.start()

    @pl.when(me > 0)
    def _():
        for copy in downs:
            copy.start()
    forward = pltpu.make_async_remote_copy(
        src_ref=gathered.at[core],
        dst_ref=gathered.at[core],
        send_sem=pass_sem.at[0],
        recv_sem=pass_sem.at[1],
        device_id=(sibling,),
        device_id_type=MESH,
    )

    def self_pair(i, _):
        leaf = 2 * i
        after = jnp.minimum(leaf + 2, last)
        fetch = [(sources.at[k], targets[k]) for k in (leaf, leaf + 1, after)]
        beside = {
            (0, 0): lambda: (mirror(ks[1], half)),
            (0, 2): lambda: (mirror(ks[0], 0)),
            (0, 3): lambda: (late(ks[1], jnp.maximum(leaf - 1, 0))),
            (0, 5): lambda: (early(ks[0], leaf)),
            (1, 0): lambda: (mirror(ks[0], half)),
            (1, 2): lambda: (mirror(ks[1], 0)),
            (1, 3): lambda: (late(ks[0], leaf)),
            (1, 5): lambda: (early(ks[1], leaf + 1)),
        }
        pipeline(chunks, AHEAD_UP, fetch, xs, ks, beside)
        return 0

    most = leaves // 2 - leaves // 8
    lax.fori_loop(0, most, self_pair, 0)
    mine.wait()
    others = gathered.at[core, pl.ds(0, chips - 1)]
    for sem in (send_sem, recv_sem):
        pltpu.make_async_copy(others, others, sem).wait()
    forward.start()
    lax.fori_loop(most, leaves // 2, self_pair, 0)
    mirror(ks[1], half)
    late(ks[1], last)
    for keep in keeps:
        keep.wait()
    forward.wait()

    @pl.when(me < n - 1)
    def _():
        for copy in ups:
            copy.wait_send()
        for copy in downs:
            copy.wait_recv()

    @pl.when(me > 0)
    def _():
        for copy in ups:
            copy.wait_recv()
        for copy in downs:
            copy.wait_send()


def down_kernel(
    near_list,
    near_count,
    far_mid,
    far_mid_count,
    far_top,
    far_top_count,
    coords,
    charges,
    before_c,
    before_q,
    after_c,
    after_q,
    gathered,
    top,
    proxy_mid,
    proxy_top,
    own_hbm,
    up_hbm,
    bases_hbm,
    sources_hbm,
    targets_hbm,
    out,
    own,
    up,
    bases,
    sources,
    targets,
    x_a,
    x_b,
    kh_a,
    kl_a,
    kh_b,
    kl_b,
    acc,
    pair_leaf,
    pair_source,
    win_q,
    mid_t,
    src_pts,
    src_q,
    bases_sem,
):
    me = lax.axis_index("leaf")
    _, leaves, points = coords.shape
    ranks = bases.shape[1]
    nodes = top.shape[0]
    vectors = charges.shape[1]
    slots = far_mid.shape[0]
    top_slots = far_top.shape[1]
    window = leaves + 2 * EDGE
    fetches = [
        pltpu.make_async_copy(src, dst, bases_sem.at[i])
        for i, (src, dst) in enumerate(
            (
                (sources_hbm, sources.at[pl.ds(EDGE, leaves)]),
                (targets_hbm, targets),
                (bases_hbm, bases),
                (up_hbm, up),
                (own_hbm, own),
            )
        )
    ]
    for fetch in fetches:
        fetch.start()

    def outside(i, _):
        for u in range(2):
            sources[2 * i + u] = source_rows(factors(before_c[:, 2 * i + u])[0])
            sources[EDGE + leaves + 2 * i + u] = source_rows(factors(after_c[:, 2 * i + u])[0])
        return 0

    lax.fori_loop(0, EDGE // 2, outside, 0)
    lane = lax.broadcasted_iota(jnp.int32, sources.shape[1:], 1)
    sources[window] = jnp.where(lane == 3, 8.0, 0.0).astype(bf16)
    win_q[0:EDGE] = before_q[...]
    win_q[EDGE : EDGE + leaves] = charges[...]
    win_q[EDGE + leaves : window] = after_q[...]
    win_q[window] = jnp.zeros_like(win_q[window])

    def coupled(target, live_slots, point_of, coeff_of, live):
        for j in range(live_slots):
            at = slice(j * ranks, (j + 1) * ranks)
            src_pts[0:3, at] = point_of(j) * UNIT
            src_q[:, at] = jnp.where(j < live, coeff_of(j), 0.0)
        cols = columns_of(target * UNIT)
        wide = live_slots * ranks
        total = jnp.zeros((2 * vectors, ranks), f32)
        step = min(512, wide)
        for lo in range(0, wide, step):
            at = slice(lo, min(lo + step, wide))
            k = weights([cols[:, i : i + 1] for i in range(3)], [src_pts[i : i + 1, at] for i in range(3)])
            kh, kl = halves(k)
            q2 = stacked(src_q[:, at])
            total = total + mm16(q2, kh, NT) + mm16(q2, kl, NT)
        return folded(total)

    per_top = FAN // nodes
    parent = (me * nodes) // FAN

    def top_coeff(j):
        s = far_top[parent, j]
        held = [s * per_top + i for i in range(per_top)]
        parts = [gathered[lax.rem(d, 2), d // 2, vectors : 2 * vectors, 0:ranks] for d in held]
        return functools.reduce(jnp.add, parts)

    top_field = coupled(
        proxy_top[:, parent],
        top_slots,
        lambda j: proxy_top[:, far_top[parent, j]],
        top_coeff,
        far_top_count[parent],
    )
    for p in range(nodes):
        node = me * nodes + p

        def mid_coeff(j):
            s = far_mid[j, node]
            d = s // nodes
            both = gathered[lax.rem(d, 2), d // 2, 0:vectors]
            out = both[:, 0:ranks]
            for i in range(1, nodes):
                out = jnp.where(s % nodes == i, both[:, i * ranks : (i + 1) * ranks], out)
            return out

        far = coupled(
            proxy_mid[:, node],
            slots,
            lambda j: proxy_mid[:, far_mid[j, node]],
            mid_coeff,
            far_mid_count[node],
        )
        mid_t[p] = far + mm(top_field, top[p])
    first = me * leaves - EDGE
    pair_leaf[0] = 0
    pair_source[0] = window

    def enlist(leaf, at):
        for j in range(1, near_list.shape[0]):
            pair_leaf[at] = leaf
            pair_source[at] = near_list[j, leaf] - first
            at = at + (j < near_count[leaf]).astype(jnp.int32)
        return at

    total = lax.fori_loop(0, leaves, enlist, 1)
    for i in range(4):
        pair_leaf[total + i] = 0
        pair_source[total + i] = window

    half = points // 2
    chunks = [(c, c + 64, 0, points) for c in range(0, points, 64)]
    xs, ks = (x_a, x_b), ((kh_a, kl_a), (kh_b, kl_b))

    def product(k_refs, i, rows):
        q2 = stacked(win_q[pair_source[i]])[:, rows]
        acc[pair_leaf[i]] += mm16(q2, k_refs[0][rows]) + mm16(q2, k_refs[1][rows])

    top_rows, low_rows = slice(0, half), slice(half, points)
    for fetch in fetches[:2]:
        fetch.wait()
    trips = total // 2

    def near(clamp):
        acc[...] = jnp.zeros_like(acc)
        kh_b[...] = jnp.zeros_like(kh_b)
        kl_b[...] = jnp.zeros_like(kl_b)
        for chunk in chunks[:AHEAD]:
            measure(x_a, sources.at[pair_source[1]], targets[pair_leaf[1]], chunk, clamp)

        def pair(i, _):
            at = 2 * i + 1
            fetch = [(sources.at[pair_source[k]], targets[pair_leaf[k]]) for k in (at, at + 1, at + 2)]
            beside = {
                (0, 0): lambda: product(ks[1], at - 1, low_rows),
                (0, 4): lambda: product(ks[0], at, top_rows),
                (1, 0): lambda: product(ks[0], at, low_rows),
                (1, 4): lambda: product(ks[1], at + 1, top_rows),
            }
            pipeline(chunks, AHEAD, fetch, xs, ks, beside, clamp)
            return 0

        lax.fori_loop(0, trips, pair, 0)
        product(ks[1], 2 * trips, low_rows)

    near(False)
    whole = functools.reduce(jnp.add, [acc[leaf] for leaf in range(leaves)])
    broken = jnp.sum(jnp.where(whole == whole, 0.0, 1.0))
    for fetch in fetches[2:]:
        fetch.wait()
    fields = [mm(mid_t[leaf // FAN], up[leaf]) for leaf in range(leaves)]
    for leaf in range(leaves):
        own[leaf] += mm(fields[leaf], bases[leaf])

    @pl.when(broken > 0.0)
    def _():
        near(True)

    for leaf in range(leaves):
        out[leaf] = (own[leaf] + folded(acc[leaf])) * out_scale


def shards(
    coords,
    charges,
    bases,
    up_transfer,
    top_transfer,
    proxy_mid,
    proxy_top,
    near_list,
    near_count,
    far_mid,
    far_mid_count,
    far_top,
    far_top_count,
):
    n = lax.axis_size("leaf")
    leaves, vectors, points = charges.shape
    ranks = bases.shape[1]
    nodes = top_transfer.shape[0]
    vmem = pl.BlockSpec(memory_space=pltpu.VMEM)
    smem = pl.BlockSpec(memory_space=pltpu.SMEM)
    anywhere = pl.BlockSpec(memory_space=pl.ANY)
    like = jax.ShapeDtypeStruct
    coords, proxy_mid, proxy_top = (x.transpose(1, 0, 2) for x in (coords, proxy_mid, proxy_top))
    near_list, far_mid = near_list.T, far_mid.T
    edge_c, edge_q = like((3, EDGE, points), f32), like((EDGE, vectors, points), f32)
    *edges, gathered, own, sources, targets = pl.pallas_call(
        functools.partial(up_kernel, n),
        out_shape=[
            edge_c,
            edge_q,
            edge_c,
            edge_q,
            like((2, n // 2, 2 * vectors, nodes * ranks), f32),
            like((leaves, vectors, points), f32),
            like((leaves, points, ROWS), bf16),
            like((leaves, ROWS, points), bf16),
        ],
        in_specs=[vmem] * 2 + [anywhere] * 3,
        out_specs=[anywhere] * 5 + [vmem] + [anywhere] * 2,
        scratch_shapes=[
            pltpu.VMEM(bases.shape, f32),
            pltpu.VMEM(up_transfer.shape, f32),
            pltpu.VMEM(top_transfer.shape, f32),
            pltpu.SemaphoreType.DMA((3,)),
            pltpu.VMEM((2 * vectors, nodes * ranks), f32),
            pltpu.VMEM((leaves, points, ROWS), bf16),
            pltpu.VMEM((leaves, ROWS, points), bf16),
            pltpu.VMEM((points, points), f32),
            pltpu.VMEM((points, points), f32),
            pltpu.VMEM((points, points), bf16),
            pltpu.VMEM((points, points), bf16),
            pltpu.VMEM((points, points), bf16),
            pltpu.VMEM((points, points), bf16),
            pltpu.SemaphoreType.DMA,
            pltpu.SemaphoreType.DMA,
            pltpu.SemaphoreType.DMA((4,)),
            pltpu.SemaphoreType.DMA((4,)),
            pltpu.SemaphoreType.DMA((3,)),
            pltpu.SemaphoreType.DMA((2,)),
        ],
        compiler_params=pltpu.CompilerParams(
            collective_id=0, has_side_effects=True, vmem_limit_bytes=60 << 20
        ),
        name="upward",
    )(coords, charges, bases, up_transfer, top_transfer)
    window = leaves + 2 * EDGE
    return pl.pallas_call(
        down_kernel,
        out_shape=like((leaves, vectors, points), f32),
        in_specs=[smem] * 6 + [vmem] * 10 + [anywhere] * 5,
        out_specs=vmem,
        scratch_shapes=[
            pltpu.VMEM((leaves, vectors, points), f32),
            pltpu.VMEM(up_transfer.shape, f32),
            pltpu.VMEM((leaves, ranks, points), f32),
            pltpu.VMEM((window + 1, points, ROWS), bf16),
            pltpu.VMEM((leaves, ROWS, points), bf16),
            pltpu.VMEM((points, points), f32),
            pltpu.VMEM((points, points), f32),
            pltpu.VMEM((points, points), bf16),
            pltpu.VMEM((points, points), bf16),
            pltpu.VMEM((points, points), bf16),
            pltpu.VMEM((points, points), bf16),
            pltpu.VMEM((leaves, 2 * vectors, points), f32),
            pltpu.SMEM((leaves * (near_list.shape[0] - 1) + 4,), jnp.int32),
            pltpu.SMEM((leaves * (near_list.shape[0] - 1) + 4,), jnp.int32),
            pltpu.VMEM((window + 1, vectors, points), f32),
            pltpu.VMEM((nodes, vectors, ranks), f32),
            pltpu.VMEM((8, far_mid.shape[0] * ranks), f32),
            pltpu.VMEM((vectors, far_mid.shape[0] * ranks), f32),
            pltpu.SemaphoreType.DMA((5,)),
        ],
        compiler_params=pltpu.CompilerParams(vmem_limit_bytes=60 << 20),
        name="downward",
    )(
        near_list,
        near_count,
        far_mid,
        far_mid_count,
        far_top,
        far_top_count,
        coords,
        charges,
        *edges,
        gathered,
        top_transfer,
        proxy_mid,
        proxy_top,
        own,
        up_transfer,
        bases,
        sources,
        targets,
    )


def solution(mesh):
    placed = (
        P("leaf", None, None),
        P("leaf", None, None),
        P("leaf", None, None),
        P("leaf", None, None),
        P("leaf", None, None),
        P(),
        P(),
        P("leaf", None),
        P("leaf"),
        P(),
        P(),
        P(),
        P(),
    )
    return jax.shard_map(
        shards, mesh=mesh, in_specs=placed, out_specs=P("leaf", None, None), check_vma=False
    )
```

```python
import functools

import jax
import jax.numpy as jnp
from jax import lax
from jax.experimental import pallas as pl
from jax.experimental.pallas import tpu as pltpu
from jax.sharding import PartitionSpec as P

EDGE = 8
FAN = 8
length_scale = 0.4
out_scale = 0.125
MESH = pl.DeviceIdType.MESH
TINY = 1e-30
UNIT = 1.4426950408889634 / length_scale
ROWS = 32
AHEAD = 3
AHEAD_UP = 2
f32, bf16 = jnp.float32, jnp.bfloat16
NT = (((1,), (1,)), ((), ()))
NN = (((1,), (0,)), ((), ()))


def mm16(a, b, dims=NN):
    return lax.dot_general(a, b, dims, preferred_element_type=f32)


def halves(x):
    hi = x.astype(bf16)
    return hi, (x - hi.astype(f32)).astype(bf16)


def stacked(x):
    hi = x.astype(bf16).astype(f32)
    return jnp.concatenate([hi, x - hi], axis=0).astype(bf16)


def mm(a, b, dims=NN):
    bh, bl = halves(b)
    return folded(mm16(stacked(a), bh, dims)) + mm16(a.astype(bf16), bl, dims)


def folded(x):
    rows = x.shape[0] // 2
    return x[:rows] + x[rows:]


def decay(x):
    return jnp.exp2(-(x * lax.rsqrt(x)))


def weights(cols, rows):
    dx, dy, dz = (c - r for c, r in zip(cols, rows))
    return decay(jnp.maximum(dx * dx + dy * dy + dz * dz, TINY))


def columns_of(pts):
    pad = jnp.zeros((8 - pts.shape[0], pts.shape[1]), f32)
    return jnp.concatenate([pts, pad], axis=0).T


def rounded(x):
    return x.astype(bf16).astype(f32)


def pieces(x, count):
    out = []
    for _ in range(count):
        out.append(rounded(x))
        x = x - out[-1]
    return out


def factors(pts):
    points = pts.shape[1]
    blank = jnp.full((1, points), 0.5, f32)
    at = lax.broadcasted_iota(jnp.int32, (8, points), 0)
    u = (jnp.concatenate([pts, blank, pts, blank], axis=0) - 0.5) * UNIT
    hi = jnp.floor(u * 64.0 + 0.5) * (1.0 / 64.0)
    rest = rounded(u - hi)
    upper = at < 4
    twice = hi + hi
    norm = jnp.sum(jnp.where(upper, hi * hi, 0.0), axis=0, keepdims=True)
    cross = jnp.sum(jnp.where(upper, (twice + rest) * rest, 0.0), axis=0, keepdims=True)
    n1, n2 = pieces(norm, 2)
    a1, a2, a3 = pieces(cross, 3)
    third, last = at == 3, at == 7
    fifth, five = at == 5, at < 5
    down = jnp.where(third | last, 1.0, jnp.where(upper, -twice, -2.0 * rest))
    source = [
        jnp.where(third, n1, jnp.where(last, n2, hi)),
        jnp.where(third, a1, jnp.where(last, a2, rest)),
        jnp.where(five, 1.0, jnp.where(fifth, a3, 0.0)),
        jnp.zeros_like(u),
    ]
    low = jnp.where(at == 2, a1, jnp.where(at == 3, a2, jnp.where(at == 4, a3, jnp.where(fifth, 1.0, 0.0))))
    target = [down, down, jnp.where(at == 0, n1, jnp.where(at == 1, n2, low)), jnp.zeros_like(u)]
    return source, target


def source_rows(parts):
    return jnp.concatenate(parts, axis=0).astype(bf16).T


def target_rows(parts):
    return jnp.concatenate(parts, axis=0).astype(bf16)


def measure(dst, src, tgt, chunk, clamp=True):
    start, stop, lo, hi = chunk
    x = mm16(src[start:stop, :], tgt[:, lo:hi])
    dst[start:stop, lo:hi] = jnp.maximum(x, TINY) if clamp else x


def settle(x_ref, k_refs, chunk):
    start, stop, lo, hi = chunk
    kh, kl = halves(decay(x_ref[start:stop, lo:hi]))
    k_refs[0][start:stop, lo:hi] = kh
    k_refs[1][start:stop, lo:hi] = kl


def pipeline(chunks, ahead, fetch, xs, ks, beside, clamp=True):
    n = len(chunks)
    for j in range(2 * n):
        b, c = divmod(j + ahead, n)
        measure(xs[b % 2], *fetch[b], chunks[c], clamp)
        b, c = divmod(j, n)
        if (b, c) in beside:
            beside[b, c]()
        settle(xs[b], ks[b], chunks[c])


def up_kernel(
    n,
    coords,
    charges,
    bases_hbm,
    up_hbm,
    top_hbm,
    before_c,
    before_q,
    after_c,
    after_q,
    gathered,
    own,
    sources_hbm,
    targets_hbm,
    bases,
    up,
    top,
    load_sem,
    msg,
    sources,
    targets,
    x_a,
    x_b,
    kh_a,
    kl_a,
    kh_b,
    kl_b,
    send_sem,
    recv_sem,
    halo_send,
    halo_recv,
    own_sem,
    pass_sem,
):
    me = lax.axis_index("leaf")
    _, leaves, points = coords.shape
    ranks = bases.shape[1]
    nodes = top.shape[0]
    vectors = charges.shape[1]
    barrier = pltpu.get_barrier_semaphore()

    chips = n // 2
    core, chip = lax.rem(me, 2), me // 2
    sibling = me + 1 - 2 * core
    outer = lax.rem(me + n - 1 + 2 * core, n)

    def peer(o):
        return 2 * lax.rem(chip + o, chips) + core

    def hail(to):
        pl.semaphore_signal(barrier, inc=1, device_id=(to,), device_id_type=MESH)

    def greet(o, _):
        hail(peer(o))
        return 0

    hail(sibling)
    hail(outer)
    lax.fori_loop(1, chips, greet, 0)
    loads = [
        pltpu.make_async_copy(src, dst, load_sem.at[i])
        for i, (src, dst) in enumerate(((bases_hbm, bases), (up_hbm, up), (top_hbm, top)))
    ]
    for load in loads:
        load.start()

    def halo(i, src, dst, to):
        return pltpu.make_async_remote_copy(
            src_ref=src,
            dst_ref=dst,
            send_sem=halo_send.at[i],
            recv_sem=halo_recv.at[i],
            device_id=(to,),
            device_id_type=MESH,
        )

    nxt, prv = lax.rem(me + 1, n), lax.rem(me + n - 1, n)
    tail, head = pl.ds(leaves - EDGE, EDGE), pl.ds(0, EDGE)
    ups = [
        halo(0, coords.at[:, tail], before_c, nxt),
        halo(1, charges.at[tail], before_q, nxt),
    ]
    downs = [
        halo(2, coords.at[:, head], after_c, prv),
        halo(3, charges.at[head], after_q, prv),
    ]

    def prepare(leaf):
        source, target = factors(coords[:, leaf])
        sources[leaf] = source_rows(source)
        targets[leaf] = target_rows(target)

    def prepare_some(i, _):
        for u in range(4):
            prepare(4 * i + u)
        return 0

    before = leaves // 2
    lax.fori_loop(0, before // 4, prepare_some, 0)
    msg[...] = jnp.zeros_like(msg)
    for load in loads:
        load.wait()
    for leaf in range(before, leaves):
        prepare(leaf)
    coeffs = [mm(charges[leaf], bases[leaf], NT) for leaf in range(leaves)]
    raised = [mm(coeffs[leaf], up[leaf], NT) for leaf in range(leaves)]
    mids = [functools.reduce(jnp.add, raised[p * FAN : (p + 1) * FAN]) for p in range(nodes)]
    lift = functools.reduce(jnp.add, [mm(mids[p], top[p], NT) for p in range(nodes)])
    for p in range(nodes):
        msg[0:vectors, p * ranks : (p + 1) * ranks] = mids[p]
    msg[vectors : 2 * vectors, 0:ranks] = lift
    keeps = [
        pltpu.make_async_copy(src, dst, own_sem.at[1 + i])
        for i, (src, dst) in enumerate(((sources, sources_hbm), (targets, targets_hbm)))
    ]
    for keep in keeps:
        keep.start()
    half = points // 2
    last = leaves - 1
    quarter = points // 4
    chunks = [(c, c + 64, c // quarter * quarter, points) for c in range(0, half, 64)]
    chunks += [(c, c + quarter, c, points) for c in range(half, points, quarter)]
    xs, ks = (x_a, x_b), ((kh_a, kl_a), (kh_b, kl_b))

    def mirror(k_refs, at):
        here, there = slice(at, at + quarter), slice(at + quarter, at + 2 * quarter)
        for ref in k_refs:
            ref[there, here] = ref[here, there].T

    def early(k_refs, leaf):
        q2 = stacked(charges[leaf])
        q_lo, q_hi = q2[:, :half], q2[:, half:]
        lo = hi = None
        for ref in k_refs:
            cross = ref[:half, half:]
            a = mm16(q_lo, ref[:half, :half]) + mm16(q_hi, cross, NT)
            b = mm16(q_lo, cross)
            lo, hi = (a, b) if lo is None else (lo + a, hi + b)
        own[leaf, :, :half] = folded(lo)
        own[leaf, :, half:] = folded(hi)

    def late(k_refs, leaf):
        q_hi = stacked(charges[leaf])[:, half:]
        hi = mm16(q_hi, k_refs[0][half:, half:]) + mm16(q_hi, k_refs[1][half:, half:])
        own[leaf, :, half:] += folded(hi)

    kh_b[...] = jnp.zeros_like(kh_b)
    kl_b[...] = jnp.zeros_like(kl_b)
    own[0] = jnp.zeros_like(own[0])
    for chunk in chunks[:AHEAD_UP]:
        measure(x_a, sources.at[0], targets[0], chunk)

    def send(o, _):
        pltpu.make_async_remote_copy(
            src_ref=msg,
            dst_ref=gathered.at[core, chip],
            send_sem=send_sem,
            recv_sem=recv_sem,
            device_id=(peer(o),),
            device_id_type=MESH,
        ).start()
        return 0

    pl.semaphore_wait(barrier, chips + 1)
    lax.fori_loop(1, chips, send, 0)
    mine = pltpu.make_async_copy(msg, gathered.at[core, chip], own_sem.at[0])
    mine.start()

    @pl.when(me < n - 1)
    def _():
        for copy in ups:
            copy.start()

    @pl.when(me > 0)
    def _():
        for copy in downs:
            copy.start()
    forward = pltpu.make_async_remote_copy(
        src_ref=gathered.at[core],
        dst_ref=gathered.at[core],
        send_sem=pass_sem.at[0],
        recv_sem=pass_sem.at[1],
        device_id=(sibling,),
        device_id_type=MESH,
    )

    def self_pair(i, _):
        leaf = 2 * i
        after = jnp.minimum(leaf + 2, last)
        fetch = [(sources.at[k], targets[k]) for k in (leaf, leaf + 1, after)]
        beside = {
            (0, 0): lambda: (mirror(ks[1], half)),
            (0, 2): lambda: (mirror(ks[0], 0)),
            (0, 3): lambda: (late(ks[1], jnp.maximum(leaf - 1, 0))),
            (0, 5): lambda: (early(ks[0], leaf)),
            (1, 0): lambda: (mirror(ks[0], half)),
            (1, 2): lambda: (mirror(ks[1], 0)),
            (1, 3): lambda: (late(ks[0], leaf)),
            (1, 5): lambda: (early(ks[1], leaf + 1)),
        }
        pipeline(chunks, AHEAD_UP, fetch, xs, ks, beside)
        return 0

    most = leaves // 2 - leaves // 8
    lax.fori_loop(0, most, self_pair, 0)
    mine.wait()
    others = gathered.at[core, pl.ds(0, chips - 1)]
    for sem in (send_sem, recv_sem):
        pltpu.make_async_copy(others, others, sem).wait()
    forward.start()
    lax.fori_loop(most, leaves // 2, self_pair, 0)
    mirror(ks[1], half)
    late(ks[1], last)
    for keep in keeps:
        keep.wait()
    forward.wait()

    @pl.when(me < n - 1)
    def _():
        for copy in ups:
            copy.wait_send()
        for copy in downs:
            copy.wait_recv()

    @pl.when(me > 0)
    def _():
        for copy in ups:
            copy.wait_recv()
        for copy in downs:
            copy.wait_send()


def down_kernel(
    near_list,
    near_count,
    far_mid,
    far_mid_count,
    far_top,
    far_top_count,
    coords,
    charges,
    before_c,
    before_q,
    after_c,
    after_q,
    gathered,
    top,
    proxy_mid,
    proxy_top,
    own_hbm,
    up_hbm,
    bases_hbm,
    sources_hbm,
    targets_hbm,
    out,
    own,
    up,
    bases,
    sources,
    targets,
    x_a,
    x_b,
    kh_a,
    kl_a,
    kh_b,
    kl_b,
    acc,
    pair_leaf,
    pair_source,
    win_q,
    mid_t,
    src_pts,
    src_q,
    bases_sem,
):
    me = lax.axis_index("leaf")
    _, leaves, points = coords.shape
    ranks = bases.shape[1]
    nodes = top.shape[0]
    vectors = charges.shape[1]
    slots = far_mid.shape[0]
    top_slots = far_top.shape[1]
    window = leaves + 2 * EDGE
    fetches = [
        pltpu.make_async_copy(src, dst, bases_sem.at[i])
        for i, (src, dst) in enumerate(
            (
                (sources_hbm, sources.at[pl.ds(EDGE, leaves)]),
                (targets_hbm, targets),
                (bases_hbm, bases),
                (up_hbm, up),
                (own_hbm, own),
            )
        )
    ]
    for fetch in fetches:
        fetch.start()

    lane = lax.broadcasted_iota(jnp.int32, sources.shape[1:], 1)
    sources[window] = jnp.where(lane == 3, 8.0, 0.0).astype(bf16)
    win_q[0:EDGE] = before_q[...]
    win_q[EDGE : EDGE + leaves] = charges[...]
    win_q[EDGE + leaves : window] = after_q[...]
    win_q[window] = jnp.zeros_like(win_q[window])

    def coupled(target, live_slots, point_of, coeff_of, live):
        for j in range(live_slots):
            at = slice(j * ranks, (j + 1) * ranks)
            src_pts[0:3, at] = point_of(j) * UNIT
            src_q[:, at] = jnp.where(j < live, coeff_of(j), 0.0)
        cols = columns_of(target * UNIT)
        wide = live_slots * ranks
        total = jnp.zeros((2 * vectors, ranks), f32)
        step = min(512, wide)
        for lo in range(0, wide, step):
            at = slice(lo, min(lo + step, wide))
            k = weights([cols[:, i : i + 1] for i in range(3)], [src_pts[i : i + 1, at] for i in range(3)])
            kh, kl = halves(k)
            q2 = stacked(src_q[:, at])
            total = total + mm16(q2, kh, NT) + mm16(q2, kl, NT)
        return folded(total)

    per_top = FAN // nodes
    parent = (me * nodes) // FAN

    def top_coeff(j):
        s = far_top[parent, j]
        held = [s * per_top + i for i in range(per_top)]
        parts = [gathered[lax.rem(d, 2), d // 2, vectors : 2 * vectors, 0:ranks] for d in held]
        return functools.reduce(jnp.add, parts)

    top_field = coupled(
        proxy_top[:, parent],
        top_slots,
        lambda j: proxy_top[:, far_top[parent, j]],
        top_coeff,
        far_top_count[parent],
    )
    for p in range(nodes):
        node = me * nodes + p

        def mid_coeff(j):
            s = far_mid[j, node]
            d = s // nodes
            both = gathered[lax.rem(d, 2), d // 2, 0:vectors]
            out = both[:, 0:ranks]
            for i in range(1, nodes):
                out = jnp.where(s % nodes == i, both[:, i * ranks : (i + 1) * ranks], out)
            return out

        far = coupled(
            proxy_mid[:, node],
            slots,
            lambda j: proxy_mid[:, far_mid[j, node]],
            mid_coeff,
            far_mid_count[node],
        )
        mid_t[p] = far + mm(top_field, top[p])
    for i in range(EDGE):
        sources[i] = source_rows(factors(before_c[:, i])[0])
        sources[EDGE + leaves + i] = source_rows(factors(after_c[:, i])[0])
    first = me * leaves - EDGE
    pair_leaf[0] = 0
    pair_source[0] = window

    def enlist(leaf, at):
        for j in range(1, near_list.shape[0]):
            pair_leaf[at] = leaf
            pair_source[at] = near_list[j, leaf] - first
            at = at + (j < near_count[leaf]).astype(jnp.int32)
        return at

    total = lax.fori_loop(0, leaves, enlist, 1)
    for i in range(4):
        pair_leaf[total + i] = 0
        pair_source[total + i] = window

    half = points // 2
    chunks = [(c, c + 64, 0, points) for c in range(0, points, 64)]
    xs, ks = (x_a, x_b), ((kh_a, kl_a), (kh_b, kl_b))

    def product(k_refs, i, rows):
        q2 = stacked(win_q[pair_source[i]])[:, rows]
        acc[pair_leaf[i]] += mm16(q2, k_refs[0][rows]) + mm16(q2, k_refs[1][rows])

    top_rows, low_rows = slice(0, half), slice(half, points)
    for fetch in fetches[:2]:
        fetch.wait()
    trips = total // 2

    def near(clamp):
        acc[...] = jnp.zeros_like(acc)
        kh_b[...] = jnp.zeros_like(kh_b)
        kl_b[...] = jnp.zeros_like(kl_b)
        for chunk in chunks[:AHEAD]:
            measure(x_a, sources.at[pair_source[1]], targets[pair_leaf[1]], chunk, clamp)

        def pair(i, _):
            at = 2 * i + 1
            fetch = [(sources.at[pair_source[k]], targets[pair_leaf[k]]) for k in (at, at + 1, at + 2)]
            beside = {
                (0, 0): lambda: product(ks[1], at - 1, low_rows),
                (0, 4): lambda: product(ks[0], at, top_rows),
                (1, 0): lambda: product(ks[0], at, low_rows),
                (1, 4): lambda: product(ks[1], at + 1, top_rows),
            }
            pipeline(chunks, AHEAD, fetch, xs, ks, beside, clamp)
            return 0

        lax.fori_loop(0, trips, pair, 0)
        product(ks[1], 2 * trips, low_rows)

    near(False)
    whole = functools.reduce(jnp.add, [acc[leaf] for leaf in range(leaves)])
    broken = jnp.sum(jnp.where(whole == whole, 0.0, 1.0))
    for fetch in fetches[2:]:
        fetch.wait()
    fields = [mm(mid_t[leaf // FAN], up[leaf]) for leaf in range(leaves)]
    for leaf in range(leaves):
        own[leaf] += mm(fields[leaf], bases[leaf])

    @pl.when(broken > 0.0)
    def _():
        near(True)

    for leaf in range(leaves):
        out[leaf] = (own[leaf] + folded(acc[leaf])) * out_scale


def shards(
    coords,
    charges,
    bases,
    up_transfer,
    top_transfer,
    proxy_mid,
    proxy_top,
    near_list,
    near_count,
    far_mid,
    far_mid_count,
    far_top,
    far_top_count,
):
    n = lax.axis_size("leaf")
    leaves, vectors, points = charges.shape
    ranks = bases.shape[1]
    nodes = top_transfer.shape[0]
    vmem = pl.BlockSpec(memory_space=pltpu.VMEM)
    smem = pl.BlockSpec(memory_space=pltpu.SMEM)
    anywhere = pl.BlockSpec(memory_space=pl.ANY)
    like = jax.ShapeDtypeStruct
    coords, proxy_mid, proxy_top = (x.transpose(1, 0, 2) for x in (coords, proxy_mid, proxy_top))
    near_list, far_mid = near_list.T, far_mid.T
    edge_c, edge_q = like((3, EDGE, points), f32), like((EDGE, vectors, points), f32)
    *edges, gathered, own, sources, targets = pl.pallas_call(
        functools.partial(up_kernel, n),
        out_shape=[
            edge_c,
            edge_q,
            edge_c,
            edge_q,
            like((2, n // 2, 2 * vectors, nodes * ranks), f32),
            like((leaves, vectors, points), f32),
            like((leaves, points, ROWS), bf16),
            like((leaves, ROWS, points), bf16),
        ],
        in_specs=[vmem] * 2 + [anywhere] * 3,
        out_specs=[anywhere] * 5 + [vmem] + [anywhere] * 2,
        scratch_shapes=[
            pltpu.VMEM(bases.shape, f32),
            pltpu.VMEM(up_transfer.shape, f32),
            pltpu.VMEM(top_transfer.shape, f32),
            pltpu.SemaphoreType.DMA((3,)),
            pltpu.VMEM((2 * vectors, nodes * ranks), f32),
            pltpu.VMEM((leaves, points, ROWS), bf16),
            pltpu.VMEM((leaves, ROWS, points), bf16),
            pltpu.VMEM((points, points), f32),
            pltpu.VMEM((points, points), f32),
            pltpu.VMEM((points, points), bf16),
            pltpu.VMEM((points, points), bf16),
            pltpu.VMEM((points, points), bf16),
            pltpu.VMEM((points, points), bf16),
            pltpu.SemaphoreType.DMA,
            pltpu.SemaphoreType.DMA,
            pltpu.SemaphoreType.DMA((4,)),
            pltpu.SemaphoreType.DMA((4,)),
            pltpu.SemaphoreType.DMA((3,)),
            pltpu.SemaphoreType.DMA((2,)),
        ],
        compiler_params=pltpu.CompilerParams(
            collective_id=0, has_side_effects=True, vmem_limit_bytes=60 << 20
        ),
        name="upward",
    )(coords, charges, bases, up_transfer, top_transfer)
    window = leaves + 2 * EDGE
    return pl.pallas_call(
        down_kernel,
        out_shape=like((leaves, vectors, points), f32),
        in_specs=[smem] * 6 + [vmem] * 10 + [anywhere] * 5,
        out_specs=vmem,
        scratch_shapes=[
            pltpu.VMEM((leaves, vectors, points), f32),
            pltpu.VMEM(up_transfer.shape, f32),
            pltpu.VMEM((leaves, ranks, points), f32),
            pltpu.VMEM((window + 1, points, ROWS), bf16),
            pltpu.VMEM((leaves, ROWS, points), bf16),
            pltpu.VMEM((points, points), f32),
            pltpu.VMEM((points, points), f32),
            pltpu.VMEM((points, points), bf16),
            pltpu.VMEM((points, points), bf16),
            pltpu.VMEM((points, points), bf16),
            pltpu.VMEM((points, points), bf16),
            pltpu.VMEM((leaves, 2 * vectors, points), f32),
            pltpu.SMEM((leaves * (near_list.shape[0] - 1) + 4,), jnp.int32),
            pltpu.SMEM((leaves * (near_list.shape[0] - 1) + 4,), jnp.int32),
            pltpu.VMEM((window + 1, vectors, points), f32),
            pltpu.VMEM((nodes, vectors, ranks), f32),
            pltpu.VMEM((8, far_mid.shape[0] * ranks), f32),
            pltpu.VMEM((vectors, far_mid.shape[0] * ranks), f32),
            pltpu.SemaphoreType.DMA((5,)),
        ],
        compiler_params=pltpu.CompilerParams(vmem_limit_bytes=60 << 20),
        name="downward",
    )(
        near_list,
        near_count,
        far_mid,
        far_mid_count,
        far_top,
        far_top_count,
        coords,
        charges,
        *edges,
        gathered,
        top_transfer,
        proxy_mid,
        proxy_top,
        own,
        up_transfer,
        bases,
        sources,
        targets,
    )


def solution(mesh):
    placed = (
        P("leaf", None, None),
        P("leaf", None, None),
        P("leaf", None, None),
        P("leaf", None, None),
        P("leaf", None, None),
        P(),
        P(),
        P("leaf", None),
        P("leaf"),
        P(),
        P(),
        P(),
        P(),
    )
    return jax.shard_map(
        shards, mesh=mesh, in_specs=placed, out_specs=P("leaf", None, None), check_vma=False
    )
```
